32 devices in a mesh: gy: 8 (over y, x, core), gx: 4 (over z).
Axes of the slice: x: 2, y: 2, z: 4, core: 2. Of those that a mesh axis runs over, the one named last changes fastest.
Arguments:
- fields: bfloat16 [16, 1472, 2048], P(None, 'gy', 'gx'), may hold values from -6 to 6
- level_order: int32 [16], replicated, may hold values from 0 to 15, each once
- m_owner: int32 [1024], replicated, may hold values from 0 to 7, as said below
- n_count: int32 [1024], replicated, may hold values from 1 to 736, as said below
Outputs:
- spectrum: float32 [16, 1536, 2944], P('gx', 'gy')
The draws below stay inside these ranges and needn't reach their ends.
Inputs may be any that keep to these rules, and one draw needn't show every extreme that they name: `m_owner`: each owner is named by at most 192 wavenumbers m, and some owner by exactly 192. Wavenumbers n = 0 to n_count[m] - 1 are retained for m; the count for m = 0 is 736.
All inputs are finite; a program needn't handle non-finite values.
Results may differ from the reference program's by a relative error of at most 0.0066.
Values may be sent and summed in bfloat16 or wider, within the bound.
A program may use at most 64 MiB of HBM per device.

```python
import math
import jax
import jax.numpy as jnp
from jax import lax

NX = 2048
NY = 1472
LEV = 16
M = 1024
NN = 736
MCAP = 192
N_GY = 8


def draw_m_owner(key, part):
    key_full = jax.random.fold_in(key, 11)
    key_rank = jax.random.fold_in(key, 12)
    key_mode = jax.random.fold_in(key, 13)
    slot_total = N_GY * MCAP
    full_owner = jax.random.randint(key_full, (), 0, N_GY)
    slot_ranks = jax.random.permutation(key_rank, slot_total).astype(jnp.int32)
    slot_owner = jnp.arange(slot_total, dtype=jnp.int32) // MCAP
    scores = slot_ranks + jnp.where(slot_owner == full_owner, 0, slot_total).astype(jnp.int32)
    ordering = jnp.argsort(scores, stable=True)
    chosen = (ordering[:M] // MCAP).astype(jnp.int32)
    mode_perm = jax.random.permutation(key_mode, M)
    return jnp.zeros((M,), jnp.int32).at[mode_perm].set(chosen)


def draw_n_count(key, part):
    key_jitter = jax.random.fold_in(key, 21)
    scaled_m = jnp.arange(M, dtype=jnp.int32)[:, None] * 1024 // M
    scaled_n = jnp.arange(NN, dtype=jnp.int32)[None, :] * 1024 // NN
    inside = (scaled_m * scaled_m + scaled_n * scaled_n <= 1024 * 1024).astype(jnp.int32)
    ellipse = jnp.sum(inside, axis=1)
    jitter = jax.random.randint(key_jitter, (M,), 0, 17)
    return jnp.minimum(NN, ellipse + jitter).astype(jnp.int32)


def steps_of(rng, shape, split, least, top_value):
    def one(dim, shards_of):
        steps = jax.random.uniform(jax.random.fold_in(jax.random.fold_in(rng, 6), dim), (shards_of,), jnp.float32, least / len(split), top_value / len(split))
        return jnp.repeat(jnp.exp(steps), shape[dim] // shards_of).reshape((-1,) + (1,) * (len(shape) - dim - 1))

    level = one(*split[0])
    for cut in split[1:]:
        level = level * one(*cut)
    return level


def centred(own_key, dims, scale, bound, split=(), held_as=jnp.bfloat16):
    drawn = scale * jax.random.normal(own_key, dims, jnp.float32)
    if split:
        drawn = drawn * steps_of(own_key, dims, split, -0.22, 0.18)
    return jnp.clip(drawn, -bound, bound).astype(held_as)


def setup_inputs(seed: int = 0) -> dict:
    key_of = jax.random.split(jax.random.key(seed), 5)
    fields = centred(key_of[0], (LEV, NY, NX), 1.0, 6.0, ((1, 8), (2, 4)))
    level_order = jax.random.permutation(key_of[1], LEV).astype(jnp.int32)
    m_owner = draw_m_owner(jax.random.fold_in(key_of[4], 71), 0)
    n_count = draw_n_count(jax.random.fold_in(key_of[4], 71), 0)
    return {"fields": fields, "level_order": level_order, "m_owner": m_owner, "n_count": n_count}


def mode_tables(extent, mode_total):
    middle = extent // 2
    points = jnp.arange(middle + 1, dtype=jnp.int32)
    orders = jnp.arange(mode_total, dtype=jnp.int32)
    phases = (points[:, None] * orders[None, :] % extent).astype(jnp.float32) * (2.0 * math.pi / extent)
    weight = jnp.where((points == 0) | (points == middle), 0.5, 1.0).astype(jnp.float32)
    factor = 1.0 / math.sqrt(extent)
    cos_even = (weight[:, None] * jnp.cos(phases) * factor).astype(jnp.bfloat16)
    sin_odd = (-jnp.sin(phases) * factor).astype(jnp.bfloat16)
    return (cos_even, sin_odd)

def fold_ends(values, along_dim):
    extent = values.shape[along_dim]
    middle = extent // 2
    leading = lax.slice_in_dim(values, 0, middle + 1, axis=along_dim)
    anchor = lax.slice_in_dim(values, 0, 1, axis=along_dim)
    trailing = jnp.flip(lax.slice_in_dim(values, middle, extent, axis=along_dim), along_dim)
    mirror = jnp.concatenate([anchor, trailing], along_dim)
    even_part = (leading.astype(jnp.float32) + mirror.astype(jnp.float32)).astype(jnp.bfloat16)
    odd_part = (leading.astype(jnp.float32) - mirror.astype(jnp.float32)).astype(jnp.bfloat16)
    return (even_part, odd_part)

def slot_table(m_owner, groups, capacity):
    mode_count = m_owner.shape[0]
    modes = jnp.arange(mode_count, dtype=jnp.int32)
    keys = (m_owner * mode_count + modes).astype(jnp.int32)
    ordering = jnp.argsort(keys, stable=True).astype(jnp.int32)
    sorted_owner = jnp.take(m_owner, ordering).astype(jnp.int32)
    owners = jnp.arange(groups, dtype=jnp.int32)
    counts = lax.optimization_barrier(jnp.sum((m_owner[:, None] == owners[None, :]).astype(jnp.int32), axis=0)).astype(jnp.int32)
    starts = (jnp.cumsum(counts) - counts).astype(jnp.int32)
    within = (modes - jnp.take(starts, sorted_owner)).astype(jnp.int32)
    slot_index = (sorted_owner * capacity + within).astype(jnp.int32)
    slot_modes = jnp.zeros((groups * capacity,), jnp.int32).at[slot_index].set(ordering)
    filled = jnp.zeros((groups * capacity,), jnp.float32).at[slot_index].set(1.0)
    return (slot_modes, filled)

def reference(fields, level_order, m_owner, n_count):
    mode_count = NX // 2
    wave_count = NY // 2
    cos_x, sin_x = mode_tables(NX, mode_count)
    cos_y, sin_y = mode_tables(NY, wave_count)
    slot_modes, filled = slot_table(m_owner, N_GY, MCAP)
    retained = (jnp.arange(wave_count, dtype=jnp.int32)[None, :] < n_count[:, None]).astype(jnp.float32)

    def one_level(level_index):
        level_grid = fields[level_index]
        even_part, odd_part = fold_ends(level_grid, 1)
        along = jnp.dot(even_part, cos_x, preferred_element_type=jnp.float32).astype(jnp.bfloat16)
        across = jnp.dot(odd_part, sin_x, preferred_element_type=jnp.float32).astype(jnp.bfloat16)
        spectra = jnp.stack([along, across], 0)
        even_y, odd_y = fold_ends(spectra, 1)
        cosine_part = jnp.einsum('cym,yn->mcn', even_y.astype(jnp.float32), cos_y.astype(jnp.float32), precision=lax.Precision.HIGHEST)
        sine_part = jnp.einsum('cym,yn->mcn', odd_y.astype(jnp.float32), sin_y.astype(jnp.float32), precision=lax.Precision.HIGHEST)
        result = jnp.stack([cosine_part, sine_part], 2) * retained[:, None, None, :]
        picked = jnp.take(result.reshape(mode_count, 4 * wave_count), slot_modes, axis=0)
        return picked * filled[:, None]
    return lax.map(one_level, level_order)
```

```python
import functools
import math

import jax
import ml_dtypes
import numpy as np
import jax.numpy as jnp
from jax import lax
from jax.experimental import pallas as pl
from jax.experimental.pallas import tpu as pltpu
from jax.sharding import PartitionSpec as P

NX = 2048
NY = 1472
MESH = pl.DeviceIdType.MESH
COARSE = 32


def mode_tables(extent, mode_total):
    middle = extent // 2
    points = jnp.arange(middle + 1, dtype=jnp.int32)
    orders = jnp.arange(mode_total, dtype=jnp.int32)
    phases = (points[:, None] * orders[None, :] % extent).astype(jnp.float32) * (
        2.0 * math.pi / extent
    )
    weight = jnp.where((points == 0) | (points == middle), 0.5, 1.0).astype(jnp.float32)
    factor = 1.0 / math.sqrt(extent)
    cos_even = (weight[:, None] * jnp.cos(phases) * factor).astype(jnp.bfloat16)
    sin_odd = (-jnp.sin(phases) * factor).astype(jnp.bfloat16)
    return (cos_even, sin_odd)


def fold_ends(values, along_dim):
    extent = values.shape[along_dim]
    middle = extent // 2
    leading = lax.slice_in_dim(values, 0, middle + 1, axis=along_dim)
    anchor = lax.slice_in_dim(values, 0, 1, axis=along_dim)
    trailing = jnp.flip(lax.slice_in_dim(values, middle, extent, axis=along_dim), along_dim)
    mirror = jnp.concatenate([anchor, trailing], along_dim)
    even_part = (leading.astype(jnp.float32) + mirror.astype(jnp.float32)).astype(jnp.bfloat16)
    odd_part = (leading.astype(jnp.float32) - mirror.astype(jnp.float32)).astype(jnp.bfloat16)
    return (even_part, odd_part)


def slot_table(m_owner, groups, capacity):
    mode_count = m_owner.shape[0]
    modes = jnp.arange(mode_count, dtype=jnp.int32)
    keys = m_owner * mode_count + modes
    ordering = jnp.argsort(keys, stable=True)
    sorted_owner = jnp.take(m_owner, ordering)
    owners = jnp.arange(groups, dtype=jnp.int32)
    counts = jnp.sum((m_owner[:, None] == owners[None, :]).astype(jnp.int32), axis=0)
    starts = jnp.cumsum(counts) - counts
    within = modes - jnp.take(starts, sorted_owner)
    slot_index = sorted_owner * capacity + within
    slot_modes = jnp.zeros((groups * capacity,), jnp.int32).at[slot_index].set(ordering)
    filled = jnp.zeros((groups * capacity,), jnp.float32).at[slot_index].set(1.0)
    return (slot_modes, filled)


def body(fields, level_order, m_owner, n_count):
    groups_x = lax.axis_size("gx")
    groups_y = lax.axis_size("gy")
    per_set = fields.shape[0] // groups_x
    mode_count = m_owner.shape[0]
    wave_count = NY // 2
    capacity = 3 * mode_count // (2 * groups_y)
    ordered = jnp.take(fields, level_order, axis=0)
    line_data = lax.all_to_all(ordered, "gx", split_axis=0, concat_axis=2, tiled=True)
    cos_x, sin_x = mode_tables(NX, mode_count)
    even_part, odd_part = fold_ends(line_data, 2)
    along = jnp.einsum("lyx,xm->lym", even_part, cos_x, preferred_element_type=jnp.float32).astype(
        jnp.bfloat16
    )
    across = jnp.einsum("lyx,xm->lym", odd_part, sin_x, preferred_element_type=jnp.float32).astype(
        jnp.bfloat16
    )
    spectra = jnp.stack([along, across], 1)
    slot_modes, filled = slot_table(m_owner, groups_y, capacity)
    outgoing = jnp.take(spectra, slot_modes, axis=3)
    arrived = lax.all_to_all(outgoing, "gy", split_axis=3, concat_axis=2, tiled=True)
    first_slot = lax.axis_index("gy") * capacity
    own_modes = lax.dynamic_slice_in_dim(slot_modes, first_slot, capacity)
    own_filled = lax.dynamic_slice_in_dim(filled, first_slot, capacity)
    own_counts = jnp.take(n_count, own_modes)
    retained = (jnp.arange(wave_count, dtype=jnp.int32)[None, :] < own_counts[:, None]).astype(
        jnp.float32
    ) * own_filled[:, None]
    cos_y, sin_y = mode_tables(NY, wave_count)
    even_y, odd_y = fold_ends(arrived, 2)
    cosine_part = jnp.einsum("lcys,yn->lscn", even_y, cos_y, preferred_element_type=jnp.float32)
    sine_part = jnp.einsum("lcys,yn->lscn", odd_y, sin_y, preferred_element_type=jnp.float32)
    result = jnp.stack([cosine_part, sine_part], 3) * retained[None, :, None, None, :]
    return result.reshape(per_set, capacity, 4 * wave_count)


def unit_angles(products, extent):
    phases = (products % extent).astype(np.float64) * (2.0 * math.pi / extent)
    cosine = np.cos(phases)
    sine = np.where((products * 2) % extent == 0, 0.0, np.sin(phases))
    return cosine, sine


def split_x_table(extent, mode_total):
    modes = np.arange(mode_total)
    coarse = np.arange(extent // COARSE)[:, None] * COARSE * modes[None, :]
    fine = np.arange(COARSE)[:, None] * modes[None, :]
    cos_a, sin_a = unit_angles(coarse, extent)
    cos_b, sin_b = unit_angles(fine, extent)
    factor = 1.0 / math.sqrt(extent)
    rest = np.concatenate([cos_a * factor, sin_a * factor, cos_b, sin_b], 0).astype(np.float32)
    terms = []
    for _ in range(3):
        term = rest.astype(ml_dtypes.bfloat16)
        terms.append(term)
        rest = rest - term.astype(np.float32)
    return np.stack(terms, 0)


def full_y_table(extent, wave_total):
    points = np.arange(extent)[:, None]
    orders = np.arange(wave_total)[None, :]
    cosine, sine = unit_angles(points * orders, extent)
    factor = 1.0 / math.sqrt(extent)
    both = np.concatenate([cosine * factor, -sine * factor], 1).astype(np.float32)
    return both.astype(ml_dtypes.bfloat16)


def exchange_kernel(
    groups_x, groups_y, capacity, order_ref, fields_ref, owner_row_ref, owner_col_ref, count_ref,
    split_ref, out_ref, keep_ref, send_x, line, slot_col, parts, table, spectra,
    x_send_sem, x_recv_sem, y_send_sem, y_recv_sem, own_sem,
):
    me_x = lax.axis_index("gx")
    me_y = lax.axis_index("gy")
    levels, rows, width = fields_ref.shape
    per_set = levels // groups_x
    mode_count = owner_row_ref.shape[1]
    pair = 2 * capacity
    coarse_total = groups_x * width // COARSE

    barrier = pltpu.get_barrier_semaphore()
    for step in range(1, groups_x):
        pl.semaphore_signal(
            barrier, inc=1, device_id={"gx": lax.rem(me_x + step, groups_x)}, device_id_type=MESH
        )
    for step in range(1, groups_y):
        pl.semaphore_signal(
            barrier, inc=1, device_id={"gy": lax.rem(me_y + step, groups_y)}, device_id_type=MESH
        )

    def x_copy(chunk, step):
        peer = lax.rem(me_x + step, groups_x)
        return pltpu.make_async_remote_copy(
            src_ref=send_x.at[chunk, peer],
            dst_ref=line.at[chunk, me_x],
            send_sem=x_send_sem.at[chunk, step],
            recv_sem=x_recv_sem.at[chunk, step],
            device_id={"gx": peer},
            device_id_type=MESH,
        )

    def y_copy(chunk, step):
        peer = lax.rem(me_y + step, groups_y)
        return pltpu.make_async_remote_copy(
            src_ref=spectra.at[chunk, peer],
            dst_ref=out_ref.at[chunk, me_y],
            send_sem=y_send_sem.at[chunk, step],
            recv_sem=y_recv_sem.at[chunk, step],
            device_id={"gy": peer},
            device_id_type=MESH,
        )

    for chunk in range(per_set):
        for group in range(groups_x):
            send_x[chunk, group] = fields_ref[order_ref[group * per_set + chunk]]
        line[chunk, me_x] = fields_ref[order_ref[me_x * per_set + chunk]]
        if chunk == 0:
            pl.semaphore_wait(barrier, groups_x + groups_y - 2)
        for step in range(1, groups_x):
            x_copy(chunk, step).start()

    row_block = 128
    def rank_block(block, carry):
        start = pl.multiple_of(block * row_block, row_block)
        own = owner_col_ref[pl.ds(start, row_block), :]
        before = lax.broadcasted_iota(jnp.int32, (row_block, mode_count), 1)
        here = lax.broadcasted_iota(jnp.int32, (row_block, mode_count), 0) + start
        same = jnp.where((owner_row_ref[...] == own) & (before < here), 1.0, 0.0)
        rank = jnp.sum(same, axis=1, keepdims=True).astype(jnp.int32)
        slot_col[pl.ds(start, row_block), :] = own * capacity + rank
        return carry

    lax.fori_loop(0, mode_count // row_block, rank_block, 0)

    def picked(first, size):
        lane = lax.broadcasted_iota(jnp.int32, (mode_count, size), 1)
        target = first + jnp.where(lane < capacity, lane, lane - capacity)
        return jnp.where(slot_col[...] == target, 1.0, 0.0).astype(jnp.bfloat16)

    own_pick = picked(me_y * capacity, pair)
    kept = lax.dot_general(
        own_pick, count_ref[...], (((0,), (0,)), ((), ())), preferred_element_type=jnp.float32
    )
    keep_ref[...] = kept[:capacity]

    def table_of(owner, carry):
        pick = picked(owner * capacity, pair)
        small = jnp.dot(split_ref[0], pick, preferred_element_type=jnp.float32)
        small += jnp.dot(split_ref[1], pick, preferred_element_type=jnp.float32)
        small += jnp.dot(split_ref[2], pick, preferred_element_type=jnp.float32)
        cos_a = small[:coarse_total]
        sin_a = small[coarse_total : 2 * coarse_total]
        lane = lax.broadcasted_iota(jnp.int32, (coarse_total, pair), 1)
        parts[0] = jnp.where(lane < capacity, cos_a, -sin_a)
        parts[1] = jnp.where(lane < capacity, -sin_a, -cos_a)
        cos_b = small[2 * coarse_total : 2 * coarse_total + COARSE]
        sin_b = small[2 * coarse_total + COARSE :]

        def fill(a, inner):
            value = parts[0, pl.ds(a, 1), :] * cos_b + parts[1, pl.ds(a, 1), :] * sin_b
            start = pl.multiple_of(a * COARSE, COARSE)
            table[owner, pl.ds(start, COARSE), :] = value.astype(jnp.bfloat16)
            return inner

        lax.fori_loop(0, coarse_total, fill, 0)
        return carry

    lax.fori_loop(0, groups_y, table_of, 0)

    for chunk in range(per_set):
        for step in range(1, groups_x):
            x_copy(chunk, step).wait_recv()

        def transform(owner, carry):
            whole = jnp.concatenate([line[chunk, g] for g in range(groups_x)], axis=1)
            value = jnp.dot(whole, table[owner], preferred_element_type=jnp.float32)
            spectra[chunk, owner] = value.astype(jnp.bfloat16)
            return carry

        lax.fori_loop(0, groups_y, transform, 0)
        for step in range(1, groups_y):
            y_copy(chunk, step).start()
        pltpu.make_async_copy(
            spectra.at[chunk, me_y], out_ref.at[chunk, me_y], own_sem.at[chunk]
        ).start()

    for chunk in range(per_set):
        for step in range(1, groups_x):
            x_copy(chunk, step).wait_send()
        for step in range(1, groups_y):
            y_copy(chunk, step).wait()
        pltpu.make_async_copy(
            spectra.at[chunk, me_y], out_ref.at[chunk, me_y], own_sem.at[chunk]
        ).wait()


def wave_kernel(capacity, wave_count, spectra_ref, first_ref, second_ref, keep_ref, out_ref):
    turned = spectra_ref[0].T
    total = 4 * wave_count
    span = first_ref.shape[1]
    keep = keep_ref[:, 0:1]

    def kept(value, start):
        column = lax.broadcasted_iota(jnp.int32, value.shape, 1) + start
        order = column
        for part in range(1, 4):
            order = jnp.where(column >= part * wave_count, column - part * wave_count, order)
        return jnp.where(order.astype(jnp.float32) < keep, value, 0.0)

    low = jnp.dot(turned[:capacity], first_ref[...], preferred_element_type=jnp.float32)
    high = jnp.dot(turned[capacity:], second_ref[...], preferred_element_type=jnp.float32)
    edge = total - span
    out_ref[0, :, :edge] = kept(low[:, :edge], 0)
    out_ref[0, :, edge:span] = kept(low[:, edge:] + high[:, : span - edge], edge)
    out_ref[0, :, span:] = kept(high[:, span - edge :], span)


def fused_body(groups_x, groups_y, fields, level_order, m_owner, n_count):
    levels, rows, width = fields.shape
    per_set = levels // groups_x
    mode_count = m_owner.shape[0]
    wave_count = NY // 2
    capacity = 3 * mode_count // (2 * groups_y)
    pair = 2 * capacity
    extent_x = width * groups_x
    extent_y = rows * groups_y
    split = jnp.asarray(split_x_table(extent_x, mode_count))
    y_table = full_y_table(extent_y, wave_count)
    span = -(-(2 * wave_count) // 128) * 128
    gap = span - 2 * wave_count
    first = jnp.asarray(np.pad(y_table, ((0, 0), (0, gap))))
    second = jnp.asarray(np.pad(y_table, ((0, 0), (gap, 0))))
    counts = n_count.astype(jnp.int32)[:, None]
    lanes = lax.broadcasted_iota(jnp.int32, (mode_count, 128), 1)
    count_parts = jnp.where(
        lanes < 64, jnp.where(lanes == 0, counts // 8 * 8, 0), jnp.where(lanes == 64, counts % 8, 0)
    ).astype(jnp.bfloat16)
    vmem = pl.BlockSpec(memory_space=pltpu.VMEM)
    smem = pl.BlockSpec(memory_space=pltpu.SMEM)
    arrived, keep = pl.pallas_call(
        functools.partial(exchange_kernel, groups_x, groups_y, capacity),
        out_shape=(
            jax.ShapeDtypeStruct((per_set, groups_y, rows, pair), jnp.bfloat16),
            jax.ShapeDtypeStruct((capacity, 128), jnp.float32),
        ),
        in_specs=[smem, vmem, vmem, vmem, vmem, vmem],
        out_specs=(pl.BlockSpec(memory_space=pl.ANY), vmem),
        scratch_shapes=[
            pltpu.VMEM((per_set, groups_x, rows, width), jnp.bfloat16),
            pltpu.VMEM((per_set, groups_x, rows, width), jnp.bfloat16),
            pltpu.VMEM((mode_count, 1), jnp.int32),
            pltpu.VMEM((2, extent_x // COARSE, pair), jnp.float32),
            pltpu.VMEM((groups_y, extent_x, pair), jnp.bfloat16),
            pltpu.VMEM((per_set, groups_y, rows, pair), jnp.bfloat16),
            pltpu.SemaphoreType.DMA((per_set, groups_x)),
            pltpu.SemaphoreType.DMA((per_set, groups_x)),
            pltpu.SemaphoreType.DMA((per_set, groups_y)),
            pltpu.SemaphoreType.DMA((per_set, groups_y)),
            pltpu.SemaphoreType.DMA((per_set,)),
        ],
        compiler_params=pltpu.CompilerParams(
            collective_id=0, has_side_effects=True, vmem_limit_bytes=60 * 1024 * 1024
        ),
        name="exchange",
    )(level_order, fields, m_owner[None, :], m_owner[:, None], count_parts, split)
    keep = keep[:, :1] + keep[:, 64:65]
    keep = jnp.broadcast_to(keep, (capacity, 128))
    return pl.pallas_call(
        functools.partial(wave_kernel, capacity, wave_count),
        grid=(per_set,),
        out_shape=jax.ShapeDtypeStruct((per_set, capacity, 4 * wave_count), jnp.float32),
        in_specs=[
            pl.BlockSpec((1, extent_y, pair), lambda i: (i, 0, 0)),
            pl.BlockSpec((extent_y, span), lambda i: (0, 0)),
            pl.BlockSpec((extent_y, span), lambda i: (0, 0)),
            pl.BlockSpec((capacity, 128), lambda i: (0, 0)),
        ],
        out_specs=pl.BlockSpec((1, capacity, 4 * wave_count), lambda i: (i, 0, 0)),
        compiler_params=pltpu.CompilerParams(vmem_limit_bytes=60 * 1024 * 1024),
        name="waves",
    )(arrived.reshape(per_set, extent_y, pair), first, second, keep)


def solution(mesh):
    groups_x, groups_y = mesh.shape["gx"], mesh.shape["gy"]
    in_specs = (P(None, "gy", "gx"), P(), P(), P())
    out_specs = P("gx", "gy", None)

    def whole(fields, level_order, m_owner, n_count):
        levels, rows, width = fields.shape
        capacity = 3 * m_owner.shape[0] // (2 * groups_y)
        if rows % 8 == 0 and width % 128 == 0 and capacity % 64 == 0 and levels % groups_x == 0:
            return fused_body(groups_x, groups_y, fields, level_order, m_owner, n_count)
        return body(fields, level_order, m_owner, n_count)

    return jax.shard_map(whole, mesh=mesh, in_specs=in_specs, out_specs=out_specs, check_vma=False)
```
